128 devices in a mesh: half: 2 (over core), grp: 64 (over x, y, z).
Axes of the slice: x: 4, y: 4, z: 4, core: 2. Of those that a mesh axis runs over, the one named last changes fastest.
Arguments:
- weights: float32 [2, 64, 2, 8192, 128], P('half', 'grp'), may hold values from -4 to 4
- accum: float32 [2, 64, 2, 8192], P('half', 'grp'), may hold values from 0.01 to 1
- grads: float32 [128, 128, 16, 128], P(('half', 'grp')), may hold values from -24 to 24
- row_ids: int32 [128, 128, 16], P(('half', 'grp')), may hold values from 0 to 16383
- counts: int32 [128, 128], P(('half', 'grp')), may hold values from 1 to 16, as said below
Outputs:
- new_weights: float32 [2, 64, 2, 8192, 128], P('half', 'grp')
- new_accum: float32 [2, 64, 2, 8192], P('half', 'grp')
The draws below stay inside these ranges and needn't reach their ends.
Inputs may be any that keep to these rules, and one draw needn't show every extreme that they name: `counts`: A few owners, the same for all senders, receive 16 live rows from every sender; no two of them share a shard index g (owners g and 64 + g). The owner that shares its shard index with such an owner receives 16 // 2 live rows from every sender; each other count lies from 1 to 8. So the two owners of one shard index receive at most 24 live rows from one sender together, and some pair receives exactly that.
All inputs are finite; a program needn't handle non-finite values.
Results may differ from the reference program's by a relative error of at most 0.00002.
Values sent between devices are 32-bit elements; how exact they have to be, the bound alone decides.
No kernel may reach another device: no remote copies, remote signals or barrier semaphores. Data moves between devices by JAX's collectives and lax.ppermute only.
A program may use at most 128 MiB of HBM per device.

```python
import math
import jax
import jax.numpy as jnp
import numpy as np
from jax import lax

E = 128
HR = 8192
SLOTS = 16
N_GRP = 64
DEVICES = 128


heavy_owners = 8


def draw_counts(key, part):
    first, second, third = jax.random.split(jax.random.fold_in(key, 11), 3)
    groups = DEVICES // 2
    base = jax.random.randint(first, (DEVICES, DEVICES), 1, SLOTS // 2 + 1)
    ranked = jax.random.permutation(second, groups)
    heavy_group = ranked < heavy_owners
    heavy_bit = jax.random.randint(third, (groups,), 0, 2)
    owner = jnp.arange(DEVICES, dtype=jnp.int32)
    owner_half = owner // groups
    owner_group = owner % groups
    in_heavy = heavy_group[owner_group]
    heavy = in_heavy & (owner_half == heavy_bit[owner_group])
    partner = in_heavy & jnp.logical_not(heavy)
    result = jnp.where(heavy[None, :], SLOTS, jnp.where(partner[None, :], SLOTS // 2, base))
    return result.astype(jnp.int32)


def place_ends(values, stream_key, low, largest):
    longest = values.shape.index(max(values.shape))
    spots = []
    for shift in (0, 1):
        where = [jax.random.randint(jax.random.fold_in(stream_key, axis), (), 0, length) for axis, length in enumerate(values.shape)]
        where[longest] = (where[longest] + shift) % values.shape[longest]
        spots.append(tuple(where))
    return values.at[spots[0]].set(low).at[spots[1]].set(largest)


def raised(values, key, source, target, blocks, factor):
    owner, partner = [(jnp.arange(values.shape[position]) // (values.shape[position] // blocks)).reshape([-1 if axis == position else 1 for axis in range(values.ndim)]) for position in (source, target)]
    chosen = jax.random.permutation(key, blocks)[partner]
    strong = (owner == chosen) | (owner == (partner + blocks // 2) % blocks)
    return jnp.where(strong, factor * values, values)


def block_scale(rng, dims, pieces, low, high):
    def one(axis_at, parts):
        steps = jax.random.uniform(jax.random.fold_in(jax.random.fold_in(rng, 6), axis_at), (parts,), jnp.float32, low / len(pieces), high / len(pieces))
        return jnp.repeat(jnp.exp(steps), dims[axis_at] // parts).reshape((-1,) + (1,) * (len(dims) - axis_at - 1))

    factor_of = one(*pieces[0])
    for cut in pieces[1:]:
        factor_of = factor_of * one(*cut)
    return factor_of


def rank_bounds(number_of, lean):
    loads = [(1 << 20) // math.isqrt(rank ** lean) + 1 for rank in range(1, number_of + 1)]
    spread = 1 + sum(loads) // (1 << 30)
    return np.cumsum(np.array([max(1, weight // spread) for weight in loads]))


def ranked_ids(stream_key, dims, number_of, slope):
    grid = rank_bounds(number_of, slope)
    pick = jax.random.randint(jax.random.fold_in(stream_key, 1), dims, 0, int(grid[number_of - 1]))
    standing = jnp.searchsorted(jnp.asarray(grid, jnp.int32), pick, side="right")
    return jax.random.permutation(jax.random.fold_in(stream_key, 2), number_of)[standing].astype(jnp.int32)


def noise(own_key, shape, deviation, most, shards=(), kind=jnp.bfloat16):
    drawn = deviation * jax.random.normal(own_key, shape, jnp.float32)
    if shards:
        drawn = drawn * block_scale(own_key, shape, shards, -0.22, 0.18)
    return jnp.clip(drawn, -most, most).astype(kind)


def bell_draw_with(stream_key, extent, width, limit, cuts, heavy, kind=jnp.bfloat16):
    values = width * jax.random.normal(stream_key, extent, jnp.float32)
    if cuts:
        values = values * block_scale(stream_key, extent, cuts, -0.22, 0.18)
    return jnp.clip(raised(values, jax.random.fold_in(stream_key, 3), *heavy), -limit, limit).astype(kind)


def setup_inputs(seed: int = 0) -> dict:
    seeds = jax.random.split(jax.random.key(seed), 6)
    weights = noise(seeds[0], (2, N_GRP, 2, HR, E), 0.5, 4.0, ((0, 2), (1, 64)), jnp.float32)
    accum = jnp.clip(jnp.exp(math.log(1.0) - 4.6051702 * jax.random.uniform(seeds[1], (2, N_GRP, 2, HR), jnp.float32) ** block_scale(seeds[1], (2, N_GRP, 2, HR), ((0, 2), (1, 64)), -0.2, 0.2)), 0.01, 1.0)
    grads = bell_draw_with(seeds[2], (DEVICES, DEVICES, SLOTS, E), 1.0, 24.0, ((0, 128),), (0, 1, 128, 5.5), jnp.float32)
    row_ids = place_ends(ranked_ids(seeds[3], (DEVICES, DEVICES, SLOTS), 2 * HR, 2), jax.random.fold_in(seeds[3], 3), 0, (2 * HR) - 1).astype(jnp.int32)
    counts = draw_counts(jax.random.fold_in(seeds[5], 71), 0)
    return {"weights": weights, "accum": accum, "grads": grads, "row_ids": row_ids, "counts": counts}


LEARN_RATE = 0.5
EPSILON = 1e-06

def reference(weights, accum, grads, row_ids, counts):
    groups = N_GRP
    owners = 2 * groups
    moved = jnp.transpose(weights, (2, 1, 0, 3, 4)).reshape(owners, 2 * HR, E)
    moved_acc = jnp.transpose(accum, (2, 1, 0, 3)).reshape(owners, 2 * HR)
    slot_index = lax.broadcasted_iota(jnp.int32, (owners, owners, SLOTS), 2)
    live = slot_index < counts[:, :, None]
    masked = jnp.where(live[..., None], grads, jnp.zeros_like(grads))
    owner_index = lax.broadcasted_iota(jnp.int32, (owners, owners, SLOTS), 1)
    flat_rows = (owner_index * (2 * HR) + row_ids.astype(jnp.int32)).reshape(-1)
    total = jnp.zeros((owners * 2 * HR, E), jnp.float32).at[flat_rows].add(masked.reshape(-1, E))
    total = total.reshape(owners, 2 * HR, E)
    accumulated = moved_acc + lax.optimization_barrier(jnp.mean(total * total, axis=-1))
    updated = moved - LEARN_RATE * total / (jnp.sqrt(accumulated)[..., None] + EPSILON)
    return (updated.reshape(2, groups, 2, HR, E), accumulated.reshape(2, groups, 2, HR))
```

```python
import functools

import jax
import jax.numpy as jnp
from jax import lax
from jax.experimental import pallas as pl
from jax.experimental.pallas import tpu as pltpu
from jax.sharding import PartitionSpec as P

LEARN_RATE = 0.5
EPSILON = 1e-06
BLOCK = 128
CHUNK = 1024
BANKS = 2


def pack_kernel(slots, dead, grads_ref, ids_ref, counts_ref, out_ref):
    owners = ids_ref.shape[1]
    stride = slots + 1
    slot = lax.broadcasted_iota(jnp.int32, ids_ref.shape, 0)
    marked = jnp.where(slot < counts_ref[...], ids_ref[...], dead).astype(jnp.float32)
    filler = jnp.zeros((BLOCK - slots, owners), jnp.float32)
    out_ref[pl.ds(slots, owners, stride=stride), :] = jnp.concatenate([marked, filler], 0).T
    for owner in range(owners):
        out_ref[stride * owner : stride * owner + slots, :] = grads_ref[
            slots * owner : slots * (owner + 1), :
        ]


def pack(grads, ids, counts, dead):
    owners, slots, width = grads.shape
    vmem = pl.BlockSpec(memory_space=pltpu.VMEM)
    return pl.pallas_call(
        functools.partial(pack_kernel, slots, dead),
        out_shape=jax.ShapeDtypeStruct((owners * (slots + 1), width), jnp.float32),
        in_specs=[vmem] * 3,
        out_specs=vmem,
        name="pack",
    )(grads.reshape(owners * slots, width), ids.T, counts)


def update_kernel(
    slots,
    bit_ref,
    own_ref,
    got_ref,
    own_acc_ref,
    got_acc_ref,
    rows_ref,
    out_ref,
    out_acc_ref,
    table,
    *scratch,
):
    banks = scratch[:BANKS]
    ids_v, ids_s, in_sem, out_sem, ids_sem = scratch[BANKS:]
    bit = bit_ref[0]
    half_rows = own_ref.shape[1]
    width = own_ref.shape[2]
    senders = rows_ref.shape[0] // (slots + 1)
    stride = slots + 1
    per_half = half_rows // CHUNK

    def fetch(src, chunk):
        return pltpu.make_async_copy(
            src.at[bit, pl.ds((chunk % per_half) * CHUNK, CHUNK), :],
            table.at[pl.ds(chunk * CHUNK, CHUNK), :],
            in_sem.at[chunk],
        )

    wide = rows_ref[pl.ds(slots, senders, stride=stride), :].T
    ids_v[...] = wide[:slots, :].astype(jnp.int32)
    to_scalar = pltpu.make_async_copy(ids_v, ids_s, ids_sem)
    to_scalar.start()
    for top in range(2):
        for chunk in range(top * per_half, (top + 1) * per_half):

            @pl.when(bit == top)
            def _():
                fetch(own_ref, chunk).start()

            @pl.when(bit != top)
            def _():
                fetch(got_ref, chunk).start()

    zero = jnp.zeros((256, width), jnp.float32)

    def clear(step, carry):
        for bank in banks:
            bank[pl.ds(pl.multiple_of(step * 256, 256), 256), :] = zero
        return carry

    lax.fori_loop(0, 2 * half_rows // 256, clear, 0)
    to_scalar.wait()

    def gather(sender, carry):
        base = sender * stride
        for slot in range(slots):
            row = ids_s[slot, sender]
            bank = banks[slot % BANKS]
            bank[pl.ds(row, 1), :] = bank[pl.ds(row, 1), :] + rows_ref[pl.ds(base + slot, 1), :]
        return carry

    lax.fori_loop(0, senders, gather, 0)

    ones = jnp.ones((8, width), jnp.bfloat16)
    contract = (((1,), (1,)), ((), ()))

    def flush(chunk):
        return pltpu.make_async_copy(
            table.at[pl.ds(chunk * CHUNK, CHUNK), :],
            out_ref.at[pl.ds(chunk * CHUNK, CHUNK), :],
            out_sem.at[chunk],
        )

    for top in range(2):

        def finish(step, carry, top=top):
            chunk = top * per_half + step
            fetch(own_ref, chunk).wait()
            for block in range(CHUNK // BLOCK):
                start = pl.multiple_of(chunk * CHUNK + block * BLOCK, BLOCK)
                at = pl.ds(start, BLOCK)
                lanes = pl.ds(pl.multiple_of(step * CHUNK + block * BLOCK, BLOCK), BLOCK)
                total = banks[0][at, :]
                for bank in banks[1:]:
                    total = total + bank[at, :]
                square = total * total
                high = square.astype(jnp.bfloat16)
                low = (square - high.astype(jnp.float32)).astype(jnp.bfloat16)
                summed = lax.dot_general(
                    ones, high, contract, preferred_element_type=jnp.float32
                ) + lax.dot_general(ones, low, contract, preferred_element_type=jnp.float32)
                own = own_acc_ref[:, lanes]
                got = got_acc_ref[:, lanes]
                pair = jnp.where(bit == top, own, got)
                state = jnp.where(bit == 0, pair[0:1, :], pair[1:2, :])
                state = state + summed[0:1, :] * (1.0 / width)
                out_acc_ref[pl.ds(top, 1), lanes] = state
                scale = LEARN_RATE / (jnp.sqrt(state) + EPSILON)
                scale = jnp.broadcast_to(scale, (BLOCK, BLOCK)).T
                table[at, :] = table[at, :] - total * scale
            flush(chunk).start()
            return carry

        lax.fori_loop(0, per_half, finish, 0)

    for chunk in range(2 * per_half):
        flush(chunk).wait()


def update(bit, own, got, own_acc, got_acc, rows, slots):
    halves, half_rows, width = own.shape
    senders = rows.shape[0] // (slots + 1)
    chunks = halves * half_rows // CHUNK
    vmem = pl.BlockSpec(memory_space=pltpu.VMEM)
    hbm = pl.BlockSpec(memory_space=pltpu.HBM)
    smem = pl.BlockSpec(memory_space=pltpu.SMEM)
    return pl.pallas_call(
        functools.partial(update_kernel, slots),
        out_shape=(
            jax.ShapeDtypeStruct((halves * half_rows, width), jnp.float32),
            jax.ShapeDtypeStruct((halves, half_rows), jnp.float32),
        ),
        in_specs=[smem, hbm, hbm, vmem, vmem, vmem],
        out_specs=(hbm, vmem),
        scratch_shapes=[
            pltpu.VMEM((halves * half_rows, width), jnp.float32),
            *[pltpu.VMEM((halves * half_rows + 8, width), jnp.float32) for _ in range(BANKS)],
            pltpu.VMEM((slots, senders), jnp.int32),
            pltpu.SMEM((slots, senders), jnp.int32),
            pltpu.SemaphoreType.DMA((chunks,)),
            pltpu.SemaphoreType.DMA((chunks,)),
            pltpu.SemaphoreType.DMA,
        ],
        compiler_params=pltpu.CompilerParams(vmem_limit_bytes=60 * 1024 * 1024),
        name="update",
    )(bit, own, got, own_acc, got_acc, rows)


def per_device(weights, accum, grads, row_ids, counts):
    owners, slots, width = grads.shape[1:]
    halves, half_rows = weights.shape[2:4]
    swap = [(0, 1), (1, 0)]
    table = weights[0, 0]
    state = accum[0, 0]
    got = lax.ppermute(table, "half", swap)
    got_acc = lax.ppermute(state, "half", swap)
    packed = pack(grads[0], row_ids[0], counts, halves * half_rows)
    rows = lax.all_to_all(
        packed.reshape(owners, 1, (slots + 1) * width),
        ("half", "grp"),
        split_axis=0,
        concat_axis=0,
        tiled=True,
    ).reshape(owners * (slots + 1), width)
    bit = lax.axis_index("half").astype(jnp.int32).reshape(1)
    new_weights, new_accum = update(bit, table, got, state, got_acc, rows, slots)
    return (
        new_weights.reshape(1, 1, halves, half_rows, width),
        new_accum.reshape(1, 1, halves, half_rows),
    )


def solution(mesh):
    placed = (
        P("half", "grp", None, None, None),
        P("half", "grp", None, None),
        P(("half", "grp"), None, None, None),
        P(("half", "grp"), None, None),
        P(("half", "grp"), None),
    )
    return jax.shard_map(
        per_device,
        mesh=mesh,
        in_specs=placed,
        out_specs=(P("half", "grp", None, None, None), P("half", "grp", None, None)),
        check_vma=False,
    )
```

```python
import functools

import jax
import jax.numpy as jnp
from jax import lax
from jax.experimental import pallas as pl
from jax.experimental.pallas import tpu as pltpu
from jax.sharding import PartitionSpec as P

LEARN_RATE = 0.5
EPSILON = 1e-06
BLOCK = 128
CHUNK = 1024
BANKS = 2


def pack_kernel(slots, dead, grads_ref, ids_ref, counts_ref, out_ref):
    owners = ids_ref.shape[1]
    stride = slots + 1
    slot = lax.broadcasted_iota(jnp.int32, ids_ref.shape, 0)
    marked = jnp.where(slot < counts_ref[...], ids_ref[...], dead).astype(jnp.float32)
    filler = jnp.zeros((BLOCK - slots, owners), jnp.float32)
    out_ref[pl.ds(slots, owners, stride=stride), :] = jnp.concatenate([marked, filler], 0).T
    for owner in range(owners):
        out_ref[stride * owner : stride * owner + slots, :] = grads_ref[
            slots * owner : slots * (owner + 1), :
        ]


def pack(grads, ids, counts, dead):
    owners, slots, width = grads.shape
    vmem = pl.BlockSpec(memory_space=pltpu.VMEM)
    return pl.pallas_call(
        functools.partial(pack_kernel, slots, dead),
        out_shape=jax.ShapeDtypeStruct((owners * (slots + 1), width), jnp.float32),
        in_specs=[vmem] * 3,
        out_specs=vmem,
        name="pack",
    )(grads.reshape(owners * slots, width), ids.T, counts)


def update_kernel(
    slots,
    bit_ref,
    own_ref,
    got_ref,
    own_acc_ref,
    got_acc_ref,
    rows_ref,
    out_ref,
    out_acc_ref,
    table,
    *scratch,
):
    banks = scratch[:BANKS]
    ids_v, ids_s, spread_ref, in_sem, out_sem, ids_sem = scratch[BANKS:]
    bit = bit_ref[0]
    half_rows = own_ref.shape[1]
    width = own_ref.shape[2]
    senders = rows_ref.shape[0] // (slots + 1)
    stride = slots + 1
    per_half = half_rows // CHUNK
    blocks = CHUNK // BLOCK

    def fetch(src, chunk):
        return pltpu.make_async_copy(
            src.at[bit, pl.ds((chunk % per_half) * CHUNK, CHUNK), :],
            table.at[pl.ds(chunk * CHUNK, CHUNK), :],
            in_sem.at[chunk],
        )

    wide = rows_ref[pl.ds(slots, senders, stride=stride), :].T
    ids_v[...] = wide[:slots, :].astype(jnp.int32)
    to_scalar = pltpu.make_async_copy(ids_v, ids_s, ids_sem)
    to_scalar.start()
    for top in range(2):
        for chunk in range(top * per_half, (top + 1) * per_half):

            @pl.when(bit == top)
            def _():
                fetch(own_ref, chunk).start()

            @pl.when(bit != top)
            def _():
                fetch(got_ref, chunk).start()

    zero = jnp.zeros((256, width), jnp.float32)

    def clear(step, carry):
        for bank in banks:
            bank[pl.ds(pl.multiple_of(step * 256, 256), 256), :] = zero
        return carry

    lax.fori_loop(0, 2 * half_rows // 256, clear, 0)
    to_scalar.wait()

    def gather(sender, carry):
        base = sender * stride
        for slot in range(0, slots, 2):
            bank = banks[(slot // 2) % BANKS]
            first = ids_s[slot, sender]
            second = ids_s[slot + 1, sender]
            one = rows_ref[pl.ds(base + slot, 1), :]
            two = rows_ref[pl.ds(base + slot + 1, 1), :]
            two = jnp.where(first == second, one + two, two)
            held = bank[pl.ds(first, 1), :]
            other = bank[pl.ds(second, 1), :]
            bank[pl.ds(first, 1), :] = held + one
            bank[pl.ds(second, 1), :] = other + two
        return carry

    lax.fori_loop(0, senders, gather, 0, unroll=2)

    lane = lax.broadcasted_iota(jnp.int32, (BLOCK, BLOCK), 1)
    part = lax.broadcasted_iota(jnp.int32, spread_ref.shape, 0)
    column = lax.broadcasted_iota(jnp.int32, spread_ref.shape, 1)
    chosen = (part < 3 * blocks) & (part % blocks == column // BLOCK)
    spread_ref[...] = jnp.where(chosen, 1.0, 0.0).astype(jnp.bfloat16)

    def flush(chunk):
        return pltpu.make_async_copy(
            table.at[pl.ds(chunk * CHUNK, CHUNK), :],
            out_ref.at[pl.ds(chunk * CHUNK, CHUNK), :],
            out_sem.at[chunk],
        )

    def at(chunk, block):
        return pl.ds(pl.multiple_of(chunk * CHUNK + block * BLOCK, BLOCK), BLOCK)

    def total(where):
        value = banks[0][where, :]
        for bank in banks[1:]:
            value = value + bank[where, :]
        return value

    def measure(chunk):
        top = chunk // per_half
        step = chunk % per_half
        sums = jnp.zeros((BLOCK, BLOCK), jnp.float32)
        for block in range(blocks):
            value = total(at(chunk, block))
            summed = jnp.sum(value * value, axis=1, keepdims=True)
            sums = jnp.where(lane == block, summed, sums)
        picked = pl.ds(2 * blocks * step + bit, blocks, stride=2)
        state = jnp.where(bit == top, own_acc_ref[picked, :], got_acc_ref[picked, :])
        state = state + sums.T[:blocks, :] * (1.0 / width)
        out_acc_ref[pl.ds(2 * blocks * step + top, blocks, stride=2), :] = state
        return LEARN_RATE / (jnp.sqrt(state) + EPSILON)

    def apply(chunk, scale):
        high = scale.astype(jnp.bfloat16).astype(jnp.float32)
        rest = scale - high
        middle = rest.astype(jnp.bfloat16).astype(jnp.float32)
        filler = jnp.zeros((BLOCK - 3 * blocks, BLOCK), jnp.float32)
        parts = jnp.concatenate([high, middle, rest - middle, filler], 0).T
        wide = jnp.dot(
            parts.astype(jnp.bfloat16), spread_ref[...], preferred_element_type=jnp.float32
        )
        for block in range(blocks):
            where = at(chunk, block)
            factor = wide[:, block * BLOCK : (block + 1) * BLOCK]
            table[where, :] = table[where, :] - total(where) * factor

    def finish(chunk, scale):
        fetch(own_ref, chunk).wait()
        following = measure(chunk + 1)
        apply(chunk, scale)
        flush(chunk).start()
        return following

    last = 2 * per_half - 1
    scale = lax.fori_loop(0, last, finish, measure(0))
    fetch(own_ref, last).wait()
    apply(last, scale)
    flush(last).start()
    for chunk in range(2 * per_half):
        flush(chunk).wait()


def update(bit, own, got, own_acc, got_acc, rows, slots):
    halves, half_rows, width = own.shape
    senders = rows.shape[0] // (slots + 1)
    chunks = halves * half_rows // CHUNK
    vmem = pl.BlockSpec(memory_space=pltpu.VMEM)
    hbm = pl.BlockSpec(memory_space=pltpu.HBM)
    smem = pl.BlockSpec(memory_space=pltpu.SMEM)
    return pl.pallas_call(
        functools.partial(update_kernel, slots),
        out_shape=(
            jax.ShapeDtypeStruct((halves * half_rows, width), jnp.float32),
            jax.ShapeDtypeStruct(own_acc.shape, jnp.float32),
        ),
        in_specs=[smem, hbm, hbm, vmem, vmem, vmem],
        out_specs=(hbm, vmem),
        scratch_shapes=[
            pltpu.VMEM((halves * half_rows, width), jnp.float32),
            *[pltpu.VMEM((halves * half_rows + 8, width), jnp.float32) for _ in range(BANKS)],
            pltpu.VMEM((slots, senders), jnp.int32),
            pltpu.SMEM((slots, senders), jnp.int32),
            pltpu.VMEM((BLOCK, CHUNK), jnp.bfloat16),
            pltpu.SemaphoreType.DMA((chunks,)),
            pltpu.SemaphoreType.DMA((chunks,)),
            pltpu.SemaphoreType.DMA,
        ],
        compiler_params=pltpu.CompilerParams(vmem_limit_bytes=48 * 1024 * 1024),
        name="update",
    )(bit, own, got, own_acc, got_acc, rows)


def per_device(weights, accum, grads, row_ids, counts):
    owners, slots, width = grads.shape[1:]
    halves, half_rows = weights.shape[2:4]
    swap = [(0, 1), (1, 0)]
    table = weights[0, 0]
    state = accum[0, 0].reshape(halves, half_rows // BLOCK, BLOCK)
    state = state.transpose(1, 0, 2).reshape(-1, BLOCK)
    got = lax.ppermute(table, "half", swap)
    got_acc = lax.ppermute(state, "half", swap)
    packed = pack(grads[0], row_ids[0], counts, halves * half_rows)
    rows = lax.all_to_all(
        packed.reshape(owners, 1, (slots + 1) * width),
        ("half", "grp"),
        split_axis=0,
        concat_axis=0,
        tiled=True,
    ).reshape(owners * (slots + 1), width)
    bit = lax.axis_index("half").astype(jnp.int32).reshape(1)
    new_weights, new_accum = update(bit, table, got, state, got_acc, rows, slots)
    new_accum = new_accum.reshape(half_rows // BLOCK, halves, BLOCK).transpose(1, 0, 2)
    return (
        new_weights.reshape(1, 1, halves, half_rows, width),
        new_accum.reshape(1, 1, halves, half_rows),
    )


def solution(mesh):
    placed = (
        P("half", "grp", None, None, None),
        P("half", "grp", None, None),
        P(("half", "grp"), None, None, None),
        P(("half", "grp"), None, None),
        P(("half", "grp"), None),
    )
    return jax.shard_map(
        per_device,
        mesh=mesh,
        in_specs=placed,
        out_specs=(P("half", "grp", None, None, None), P("half", "grp", None, None)),
        check_vma=False,
    )
```

```python
import functools

import jax
import jax.numpy as jnp
from jax import lax
from jax.experimental import pallas as pl
from jax.experimental.pallas import tpu as pltpu
from jax.sharding import PartitionSpec as P

LEARN_RATE = 0.5
EPSILON = 1e-06
BLOCK = 128
CHUNK = 1024
PACK_STEPS = 2


def split(value):
    high = value.astype(jnp.bfloat16)
    rest = value - high.astype(jnp.float32)
    middle = rest.astype(jnp.bfloat16)
    low = (rest - middle.astype(jnp.float32)).astype(jnp.bfloat16)
    return high, middle, low


def pack_kernel(slots, dead, grads_ref, ids_ref, counts_ref, out_ref, turned, flat):
    owners = ids_ref.shape[1]
    stride = slots + 1
    group = BLOCK // slots
    step = pl.program_id(0)
    batches = grads_ref.shape[0] // BLOCK

    @pl.when(step == 0)
    def _():
        slot = lax.broadcasted_iota(jnp.int32, ids_ref.shape, 0)
        marked = jnp.where(slot < counts_ref[...], ids_ref[...], dead).astype(jnp.float32)
        filler = jnp.zeros((BLOCK - slots, owners), jnp.float32)
        turned[...] = jnp.concatenate([marked, filler], 0).T
        rows = turned[pl.ds(0, owners // group, stride=group), :]
        for part in range(1, group):
            piece = turned[pl.ds(part, owners // group, stride=group), :]
            rows = rows + pltpu.roll(piece, part * slots, 1)
        flat[...] = rows

    below = lax.broadcasted_iota(jnp.int32, (BLOCK, BLOCK), 0)
    across = lax.broadcasted_iota(jnp.int32, (BLOCK, BLOCK), 1)
    together = below // slots == across // slots
    earlier = together & (below < across)
    for batch in range(batches):
        row = flat[pl.ds(step * batches + batch, 1), :]
        wide = jnp.broadcast_to(row, (BLOCK, BLOCK))
        same = wide == wide.T
        merge = jnp.where(same & together, 1.0, 0.0).astype(jnp.bfloat16)
        seen = jnp.max(jnp.where(same & earlier, 1.0, 0.0), axis=0, keepdims=True)
        kept = jnp.where(seen > 0, float(dead), row)
        merged = jnp.zeros((BLOCK, BLOCK), jnp.float32)
        for part in split(grads_ref[batch * BLOCK : (batch + 1) * BLOCK, :]):
            merged = merged + jnp.dot(merge, part, preferred_element_type=jnp.float32)
        for owner in range(group):
            base = stride * (batch * group + owner)
            out_ref[base : base + slots, :] = merged[owner * slots : (owner + 1) * slots, :]
            out_ref[base + slots : base + stride, :] = kept


def pack(grads, ids, counts, dead):
    owners, slots, width = grads.shape
    steps = PACK_STEPS
    return pl.pallas_call(
        functools.partial(pack_kernel, slots, dead),
        grid=(steps,),
        out_shape=jax.ShapeDtypeStruct((owners * (slots + 1), width), jnp.float32),
        in_specs=[
            pl.BlockSpec((owners * slots // steps, width), lambda step: (step, 0)),
            pl.BlockSpec((slots, owners), lambda step: (0, 0)),
            pl.BlockSpec((1, owners), lambda step: (0, 0)),
        ],
        out_specs=pl.BlockSpec((owners * (slots + 1) // steps, width), lambda step: (step, 0)),
        scratch_shapes=[
            pltpu.VMEM((owners, BLOCK), jnp.float32),
            pltpu.VMEM((owners * slots // BLOCK, BLOCK), jnp.float32),
        ],
        name="pack",
    )(grads.reshape(owners * slots, width), ids.T, counts)


def update_kernel(
    slots,
    bit_ref,
    own_ref,
    got_ref,
    acc_ref,
    rows_ref,
    out_ref,
    out_acc_ref,
    table,
    bank,
    ids_v,
    ids_s,
    spread_ref,
    in_sem,
    out_sem,
    ids_sem,
):
    bit = bit_ref[0]
    place = bit_ref[1]
    half_rows = own_ref.shape[1]
    width = own_ref.shape[2]
    senders = rows_ref.shape[0] // (slots + 1)
    stride = slots + 1
    per_half = half_rows // CHUNK
    blocks = CHUNK // BLOCK

    def fetch(src, chunk):
        return pltpu.make_async_copy(
            src.at[bit, pl.ds((chunk % per_half) * CHUNK, CHUNK), :],
            table.at[pl.ds(chunk * CHUNK, CHUNK), :],
            in_sem.at[chunk],
        )

    group = BLOCK // slots
    sector = lax.broadcasted_iota(jnp.int32, (senders // group, width), 1) // slots
    found = jnp.zeros((senders // group, width), jnp.float32)
    for part in range(group):
        ids = rows_ref[pl.ds(slots + part * stride, senders // group, stride=group * stride), :]
        ids = pltpu.roll(ids, lax.rem(part + group - place, group) * slots, 1)
        found = jnp.where(sector == part, ids, found)
    ids_v[...] = found.astype(jnp.int32)
    to_scalar = pltpu.make_async_copy(ids_v, ids_s, ids_sem)
    to_scalar.start()
    for top in range(2):
        for chunk in range(top * per_half, (top + 1) * per_half):

            @pl.when(bit == top)
            def _():
                fetch(own_ref, chunk).start()

            @pl.when(bit != top)
            def _():
                fetch(got_ref, chunk).start()

    zero = jnp.zeros((256, width), jnp.float32)

    def clear(step, carry):
        bank[pl.ds(pl.multiple_of(step * 256, 256), 256), :] = zero
        return carry

    lax.fori_loop(0, 2 * half_rows // 256, clear, 0)
    part = lax.broadcasted_iota(jnp.int32, spread_ref.shape, 0)
    column = lax.broadcasted_iota(jnp.int32, spread_ref.shape, 1)
    chosen = (part < 3 * blocks) & (part % blocks == column // BLOCK)
    spread_ref[...] = jnp.where(chosen, 1.0, 0.0).astype(jnp.bfloat16)
    to_scalar.wait()

    def gather(step, carry):
        for part in range(group):
            base = (step * group + part) * stride
            targets = [ids_s[step, part * slots + slot] for slot in range(slots)]
            held = [bank[pl.ds(target, 1), :] for target in targets]
            held = [old + rows_ref[pl.ds(base + slot, 1), :] for slot, old in enumerate(held)]
            for target, new in zip(targets, held):
                bank[pl.ds(target, 1), :] = new
        return carry

    lax.fori_loop(0, senders // group, gather, 0)

    lane = lax.broadcasted_iota(jnp.int32, (BLOCK, BLOCK), 1)
    def flush(chunk):
        return pltpu.make_async_copy(
            table.at[pl.ds(chunk * CHUNK, CHUNK), :],
            out_ref.at[pl.ds(chunk * CHUNK, CHUNK), :],
            out_sem.at[chunk],
        )

    def at(chunk, block):
        return pl.ds(pl.multiple_of(chunk * CHUNK + block * BLOCK, BLOCK), BLOCK)

    def measure(chunk):
        top = chunk // per_half
        step = chunk % per_half
        sums = jnp.zeros((BLOCK, BLOCK), jnp.float32)
        for block in range(blocks):
            value = bank[at(chunk, block), :]
            summed = jnp.sum(value * value, axis=1, keepdims=True)
            sums = jnp.where(lane == block, summed, sums)
        picked = pl.ds(2 * blocks * step + top, blocks, stride=2)
        state = acc_ref[picked, :]
        state = state + sums.T[:blocks, :] * (1.0 / width)
        out_acc_ref[picked, :] = state
        return LEARN_RATE / (jnp.sqrt(state) + EPSILON)

    def apply(chunk, scale):
        filler = jnp.zeros((BLOCK - 3 * blocks, BLOCK), jnp.float32)
        parts = [part.astype(jnp.float32) for part in split(scale)]
        parts = jnp.concatenate([*parts, filler], 0).T
        wide = jnp.dot(
            parts.astype(jnp.bfloat16), spread_ref[...], preferred_element_type=jnp.float32
        )
        for block in range(blocks):
            where = at(chunk, block)
            factor = wide[:, block * BLOCK : (block + 1) * BLOCK]
            table[where, :] = table[where, :] - bank[where, :] * factor

    def finish(chunk, scale):
        fetch(own_ref, chunk).wait()
        following = measure(chunk + 1)
        apply(chunk, scale)
        flush(chunk).start()
        return following

    last = 2 * per_half - 1
    scale = lax.fori_loop(0, last, finish, measure(0))
    fetch(own_ref, last).wait()
    apply(last, scale)
    flush(last).start()
    for chunk in range(2 * per_half):
        flush(chunk).wait()


def update(place, own, got, acc, rows, slots):
    halves, half_rows, width = own.shape
    senders = rows.shape[0] // (slots + 1)
    chunks = halves * half_rows // CHUNK
    vmem = pl.BlockSpec(memory_space=pltpu.VMEM)
    hbm = pl.BlockSpec(memory_space=pltpu.HBM)
    smem = pl.BlockSpec(memory_space=pltpu.SMEM)
    return pl.pallas_call(
        functools.partial(update_kernel, slots),
        out_shape=(
            jax.ShapeDtypeStruct((halves * half_rows, width), jnp.float32),
            jax.ShapeDtypeStruct(acc.shape, jnp.float32),
        ),
        in_specs=[smem, hbm, hbm, vmem, vmem],
        out_specs=(hbm, vmem),
        scratch_shapes=[
            pltpu.VMEM((halves * half_rows, width), jnp.float32),
            pltpu.VMEM((halves * half_rows + 8, width), jnp.float32),
            pltpu.VMEM((senders * slots // width, width), jnp.int32),
            pltpu.SMEM((senders * slots // width, width), jnp.int32),
            pltpu.VMEM((BLOCK, CHUNK), jnp.bfloat16),
            pltpu.SemaphoreType.DMA((chunks,)),
            pltpu.SemaphoreType.DMA((chunks,)),
            pltpu.SemaphoreType.DMA,
        ],
        compiler_params=pltpu.CompilerParams(vmem_limit_bytes=48 * 1024 * 1024),
        name="update",
    )(place, own, got, acc, rows)


def per_device(weights, accum, grads, row_ids, counts):
    owners, slots, width = grads.shape[1:]
    halves, half_rows = weights.shape[2:4]
    swap = [(0, 1), (1, 0)]
    table = weights[0, 0]
    bit = lax.axis_index("half").astype(jnp.int32)
    state = accum[0, 0].reshape(halves, half_rows // BLOCK, BLOCK).transpose(1, 0, 2)
    got = lax.ppermute(table, "half", swap)
    got_acc = lax.ppermute(state, "half", swap)
    packed = pack(grads[0], row_ids[0], counts, halves * half_rows)
    rows = lax.all_to_all(
        packed.reshape(owners, 1, (slots + 1) * width),
        ("half", "grp"),
        split_axis=0,
        concat_axis=0,
        tiled=True,
    ).reshape(owners * (slots + 1), width)
    mine = jnp.where(bit == 0, state[:, 0], state[:, 1])
    theirs = jnp.where(bit == 0, got_acc[:, 0], got_acc[:, 1])
    acc = jnp.stack([jnp.where(bit == 0, mine, theirs), jnp.where(bit == 0, theirs, mine)], 1)
    group = BLOCK // slots
    place = jnp.stack([bit, lax.rem(lax.axis_index("grp").astype(jnp.int32), group)])
    new_weights, new_accum = update(place, table, got, acc.reshape(-1, BLOCK), rows, slots)
    new_accum = new_accum.reshape(half_rows // BLOCK, halves, BLOCK).transpose(1, 0, 2)
    return (
        new_weights.reshape(1, 1, halves, half_rows, width),
        new_accum.reshape(1, 1, halves, half_rows),
    )


def solution(mesh):
    placed = (
        P("half", "grp", None, None, None),
        P("half", "grp", None, None),
        P(("half", "grp"), None, None, None),
        P(("half", "grp"), None, None),
        P(("half", "grp"), None),
    )
    return jax.shard_map(
        per_device,
        mesh=mesh,
        in_specs=placed,
        out_specs=(P("half", "grp", None, None, None), P("half", "grp", None, None)),
        check_vma=False,
    )
```

```python
import functools

import jax
import jax.numpy as jnp
from jax import lax
from jax.experimental import pallas as pl
from jax.experimental.pallas import tpu as pltpu
from jax.sharding import PartitionSpec as P

LEARN_RATE = 0.5
EPSILON = 1e-06
BLOCK = 128
CHUNK = 1024
PACK_STEPS = 2


def split(value):
    high = value.astype(jnp.bfloat16)
    rest = value - high.astype(jnp.float32)
    middle = rest.astype(jnp.bfloat16)
    low = (rest - middle.astype(jnp.float32)).astype(jnp.bfloat16)
    return high, middle, low


def pack_kernel(slots, dead, grads_ref, ids_ref, counts_ref, out_ref, turned, flat):
    owners = ids_ref.shape[1]
    stride = slots + 1
    group = BLOCK // slots
    step = pl.program_id(0)
    batches = grads_ref.shape[0] // BLOCK

    @pl.when(step == 0)
    def _():
        slot = lax.broadcasted_iota(jnp.int32, ids_ref.shape, 0)
        marked = jnp.where(slot < counts_ref[...], ids_ref[...], dead).astype(jnp.float32)
        filler = jnp.zeros((BLOCK - slots, owners), jnp.float32)
        turned[...] = jnp.concatenate([marked, filler], 0).T
        rows = turned[pl.ds(0, owners // group, stride=group), :]
        for part in range(1, group):
            piece = turned[pl.ds(part, owners // group, stride=group), :]
            rows = rows + pltpu.roll(piece, part * slots, 1)
        flat[...] = rows

    below = lax.broadcasted_iota(jnp.int32, (BLOCK, BLOCK), 0)
    across = lax.broadcasted_iota(jnp.int32, (BLOCK, BLOCK), 1)
    together = below // slots == across // slots
    earlier = together & (below < across)
    for batch in range(batches):
        row = flat[pl.ds(step * batches + batch, 1), :]
        wide = jnp.broadcast_to(row, (BLOCK, BLOCK))
        same = wide == wide.T
        merge = jnp.where(same & together, 1.0, 0.0).astype(jnp.bfloat16)
        seen = jnp.max(jnp.where(same & earlier, 1.0, 0.0), axis=0, keepdims=True)
        kept = jnp.where(seen > 0, float(dead), row)
        merged = jnp.zeros((BLOCK, BLOCK), jnp.float32)
        for part in split(grads_ref[batch * BLOCK : (batch + 1) * BLOCK, :]):
            merged = merged + jnp.dot(merge, part, preferred_element_type=jnp.float32)
        for owner in range(group):
            base = stride * (batch * group + owner)
            out_ref[base : base + slots, :] = merged[owner * slots : (owner + 1) * slots, :]
            out_ref[base + slots : base + stride, :] = kept


def pack(grads, ids, counts, dead):
    owners, slots, width = grads.shape
    steps = PACK_STEPS
    return pl.pallas_call(
        functools.partial(pack_kernel, slots, dead),
        grid=(steps,),
        out_shape=jax.ShapeDtypeStruct((owners * (slots + 1), width), jnp.float32),
        in_specs=[
            pl.BlockSpec((owners * slots // steps, width), lambda step: (step, 0)),
            pl.BlockSpec((slots, owners), lambda step: (0, 0)),
            pl.BlockSpec((1, owners), lambda step: (0, 0)),
        ],
        out_specs=pl.BlockSpec((owners * (slots + 1) // steps, width), lambda step: (step, 0)),
        scratch_shapes=[
            pltpu.VMEM((owners, BLOCK), jnp.float32),
            pltpu.VMEM((owners * slots // BLOCK, BLOCK), jnp.float32),
        ],
        name="pack",
    )(grads.reshape(owners * slots, width), ids.T, counts)


def update_kernel(
    slots,
    own_ref,
    got_ref,
    acc_ref,
    rows_ref,
    out_ref,
    out_acc_ref,
    table,
    bank,
    states,
    ids_v,
    ids_s,
    spread_ref,
    in_sem,
    out_sem,
    ids_sem,
    acc_sem,
):
    bit = lax.axis_index("half").astype(jnp.int32)
    place = lax.rem(lax.axis_index("grp").astype(jnp.int32), BLOCK // slots)
    half_rows = own_ref.shape[1]
    width = own_ref.shape[2]
    senders = rows_ref.shape[0] // (slots + 1)
    stride = slots + 1
    per_half = half_rows // CHUNK
    blocks = CHUNK // BLOCK

    def fetch(src, chunk):
        return pltpu.make_async_copy(
            src.at[bit, pl.ds((chunk % per_half) * CHUNK, CHUNK), :],
            table.at[pl.ds(chunk * CHUNK, CHUNK), :],
            in_sem.at[chunk],
        )

    group = BLOCK // slots
    sector = lax.broadcasted_iota(jnp.int32, (senders // group, width), 1) // slots
    found = jnp.zeros((senders // group, width), jnp.float32)
    for part in range(group):
        ids = rows_ref[pl.ds(slots + part * stride, senders // group, stride=group * stride), :]
        ids = pltpu.roll(ids, lax.rem(part + group - place, group) * slots, 1)
        found = jnp.where(sector == part, ids, found)
    ids_v[...] = found.astype(jnp.int32)
    to_scalar = pltpu.make_async_copy(ids_v, ids_s, ids_sem)
    to_scalar.start()
    for top in range(2):
        for chunk in range(top * per_half, (top + 1) * per_half):

            @pl.when(bit == top)
            def _():
                fetch(own_ref, chunk).start()

            @pl.when(bit != top)
            def _():
                fetch(got_ref, chunk).start()

    zero = jnp.zeros((256, width), jnp.float32)

    def clear(step, carry):
        bank[pl.ds(pl.multiple_of(step * 256, 256), 256), :] = zero
        return carry

    lax.fori_loop(0, 2 * half_rows // 256, clear, 0)
    part = lax.broadcasted_iota(jnp.int32, spread_ref.shape, 0)
    column = lax.broadcasted_iota(jnp.int32, spread_ref.shape, 1)
    chosen = (part < 3 * blocks) & (part % blocks == column // BLOCK)
    spread_ref[...] = jnp.where(chosen, 1.0, 0.0).astype(jnp.bfloat16)
    to_scalar.wait()

    def gather(step, carry):
        for part in range(group):
            base = (step * group + part) * stride
            targets = [ids_s[step, part * slots + slot] for slot in range(slots)]
            held = [bank[pl.ds(target, 1), :] for target in targets]
            held = [old + rows_ref[pl.ds(base + slot, 1), :] for slot, old in enumerate(held)]
            for target, new in zip(targets, held):
                bank[pl.ds(target, 1), :] = new
        return carry

    lax.fori_loop(0, senders // group, gather, 0)

    lane = lax.broadcasted_iota(jnp.int32, (BLOCK, BLOCK), 1)
    def flush(chunk):
        return pltpu.make_async_copy(
            table.at[pl.ds(chunk * CHUNK, CHUNK), :],
            out_ref.at[pl.ds(chunk * CHUNK, CHUNK), :],
            out_sem.at[chunk],
        )

    def at(chunk, block):
        return pl.ds(pl.multiple_of(chunk * CHUNK + block * BLOCK, BLOCK), BLOCK)

    def measure(chunk):
        top = chunk // per_half
        step = chunk % per_half
        sums = jnp.zeros((BLOCK, BLOCK), jnp.float32)
        for block in range(blocks):
            value = bank[at(chunk, block), :]
            summed = jnp.sum(value * value, axis=1, keepdims=True)
            sums = jnp.where(lane == block, summed, sums)
        picked = pl.ds(2 * blocks * step + top, blocks, stride=2)
        state = acc_ref[picked, :]
        state = state + sums.T[:blocks, :] * (1.0 / width)
        states[picked, :] = state
        return LEARN_RATE / (jnp.sqrt(state) + EPSILON)

    def apply(chunk, scale):
        filler = jnp.zeros((BLOCK - 3 * blocks, BLOCK), jnp.float32)
        parts = [part.astype(jnp.float32) for part in split(scale)]
        parts = jnp.concatenate([*parts, filler], 0).T
        wide = jnp.dot(
            parts.astype(jnp.bfloat16), spread_ref[...], preferred_element_type=jnp.float32
        )
        for block in range(blocks):
            where = at(chunk, block)
            factor = wide[:, block * BLOCK : (block + 1) * BLOCK]
            table[where, :] = table[where, :] - bank[where, :] * factor

    def finish(chunk, scale):
        fetch(own_ref, chunk).wait()
        following = measure(chunk + 1)
        apply(chunk, scale)
        flush(chunk).start()
        return following

    last = 2 * per_half - 1
    scale = lax.fori_loop(0, last, finish, measure(0))
    states_out = pltpu.make_async_copy(states, out_acc_ref, acc_sem)
    states_out.start()
    fetch(own_ref, last).wait()
    apply(last, scale)
    flush(last).start()
    for chunk in range(2 * per_half):
        flush(chunk).wait()
    states_out.wait()


def update(own, got, acc, rows, slots):
    halves, half_rows, width = own.shape
    senders = rows.shape[0] // (slots + 1)
    chunks = halves * half_rows // CHUNK
    vmem = pl.BlockSpec(memory_space=pltpu.VMEM)
    hbm = pl.BlockSpec(memory_space=pltpu.HBM)
    return pl.pallas_call(
        functools.partial(update_kernel, slots),
        out_shape=(
            jax.ShapeDtypeStruct((halves * half_rows, width), jnp.float32),
            jax.ShapeDtypeStruct(acc.shape, jnp.float32),
        ),
        in_specs=[hbm, hbm, vmem, vmem],
        out_specs=(hbm, hbm),
        scratch_shapes=[
            pltpu.VMEM((halves * half_rows, width), jnp.float32),
            pltpu.VMEM((halves * half_rows + 8, width), jnp.float32),
            pltpu.VMEM(acc.shape, jnp.float32),
            pltpu.VMEM((senders * slots // width, width), jnp.int32),
            pltpu.SMEM((senders * slots // width, width), jnp.int32),
            pltpu.VMEM((BLOCK, CHUNK), jnp.bfloat16),
            pltpu.SemaphoreType.DMA((chunks,)),
            pltpu.SemaphoreType.DMA((chunks,)),
            pltpu.SemaphoreType.DMA,
            pltpu.SemaphoreType.DMA,
        ],
        compiler_params=pltpu.CompilerParams(vmem_limit_bytes=48 * 1024 * 1024),
        name="update",
    )(own, got, acc, rows)


def per_device(weights, accum, grads, row_ids, counts):
    owners, slots, width = grads.shape[1:]
    halves, half_rows = weights.shape[2:4]
    swap = [(0, 1), (1, 0)]
    table = weights[0, 0]
    bit = lax.axis_index("half").astype(jnp.int32)
    state = accum[0, 0].reshape(halves, half_rows // BLOCK, BLOCK).transpose(1, 0, 2)
    got = lax.ppermute(table, "half", swap)
    got_acc = lax.ppermute(state, "half", swap)
    packed = pack(grads[0], row_ids[0], counts, halves * half_rows)
    rows = lax.all_to_all(
        packed.reshape(owners, 1, (slots + 1) * width),
        ("half", "grp"),
        split_axis=0,
        concat_axis=0,
        tiled=True,
    ).reshape(owners * (slots + 1), width)
    mine = jnp.where(bit == 0, state[:, 0], state[:, 1])
    theirs = jnp.where(bit == 0, got_acc[:, 0], got_acc[:, 1])
    acc = jnp.stack([jnp.where(bit == 0, mine, theirs), jnp.where(bit == 0, theirs, mine)], 1)
    new_weights, new_accum = update(table, got, acc.reshape(-1, BLOCK), rows, slots)
    new_accum = new_accum.reshape(half_rows // BLOCK, halves, BLOCK).transpose(1, 0, 2)
    return (
        new_weights.reshape(1, 1, halves, half_rows, width),
        new_accum.reshape(1, 1, halves, half_rows),
    )


def solution(mesh):
    placed = (
        P("half", "grp", None, None, None),
        P("half", "grp", None, None),
        P(("half", "grp"), None, None, None),
        P(("half", "grp"), None, None),
        P(("half", "grp"), None),
    )
    return jax.shard_map(
        per_device,
        mesh=mesh,
        in_specs=placed,
        out_specs=(P("half", "grp", None, None, None), P("half", "grp", None, None)),
        check_vma=False,
    )
```

```python
import functools

import jax
import jax.numpy as jnp
from jax import lax
from jax.experimental import pallas as pl
from jax.experimental.pallas import tpu as pltpu
from jax.sharding import PartitionSpec as P

LEARN_RATE = 0.5
EPSILON = 1e-06
BLOCK = 128
CHUNK = 1024
PACK_STEPS = 2


def split(value):
    high = value.astype(jnp.bfloat16)
    rest = value - high.astype(jnp.float32)
    middle = rest.astype(jnp.bfloat16)
    low = (rest - middle.astype(jnp.float32)).astype(jnp.bfloat16)
    return high, middle, low


def pack_kernel(slots, dead, grads_ref, ids_ref, counts_ref, out_ref, turned, flat):
    owners = ids_ref.shape[1]
    stride = slots + 1
    group = BLOCK // slots
    step = pl.program_id(0)
    batches = grads_ref.shape[0] // BLOCK

    @pl.when(step == 0)
    def _():
        slot = lax.broadcasted_iota(jnp.int32, ids_ref.shape, 0)
        marked = jnp.where(slot < counts_ref[...], ids_ref[...], dead).astype(jnp.float32)
        filler = jnp.zeros((BLOCK - slots, owners), jnp.float32)
        turned[...] = jnp.concatenate([marked, filler], 0).T
        rows = turned[pl.ds(0, owners // group, stride=group), :]
        for part in range(1, group):
            piece = turned[pl.ds(part, owners // group, stride=group), :]
            rows = rows + pltpu.roll(piece, part * slots, 1)
        flat[...] = rows

    below = lax.broadcasted_iota(jnp.int32, (BLOCK, BLOCK), 0)
    across = lax.broadcasted_iota(jnp.int32, (BLOCK, BLOCK), 1)
    together = below // slots == across // slots
    earlier = together & (below < across)
    for batch in range(batches):
        row = flat[pl.ds(step * batches + batch, 1), :]
        wide = jnp.broadcast_to(row, (BLOCK, BLOCK))
        same = wide == wide.T
        merge = jnp.where(same & together, 1.0, 0.0).astype(jnp.bfloat16)
        seen = jnp.max(jnp.where(same & earlier, 1.0, 0.0), axis=0, keepdims=True)
        kept = jnp.where(seen > 0, float(dead), row)
        merged = jnp.zeros((BLOCK, BLOCK), jnp.float32)
        for part in split(grads_ref[batch * BLOCK : (batch + 1) * BLOCK, :]):
            merged = merged + jnp.dot(merge, part, preferred_element_type=jnp.float32)
        for owner in range(group):
            base = stride * (batch * group + owner)
            out_ref[base : base + slots, :] = merged[owner * slots : (owner + 1) * slots, :]
            out_ref[base + slots : base + stride, :] = kept


def pack(grads, ids, counts, dead):
    owners, slots, width = grads.shape
    steps = PACK_STEPS
    return pl.pallas_call(
        functools.partial(pack_kernel, slots, dead),
        grid=(steps,),
        out_shape=jax.ShapeDtypeStruct((owners * (slots + 1), width), jnp.float32),
        in_specs=[
            pl.BlockSpec((owners * slots // steps, width), lambda step: (step, 0)),
            pl.BlockSpec((slots, owners), lambda step: (0, 0)),
            pl.BlockSpec((1, owners), lambda step: (0, 0)),
        ],
        out_specs=pl.BlockSpec((owners * (slots + 1) // steps, width), lambda step: (step, 0)),
        scratch_shapes=[
            pltpu.VMEM((owners, BLOCK), jnp.float32),
            pltpu.VMEM((owners * slots // BLOCK, BLOCK), jnp.float32),
        ],
        name="pack",
    )(grads.reshape(owners * slots, width), ids.T, counts)


def update_kernel(
    slots,
    own_ref,
    got_ref,
    acc_ref,
    rows_ref,
    out_ref,
    out_acc_ref,
    table,
    bank,
    states,
    ids_v,
    ids_s,
    spread_ref,
    in_sem,
    out_sem,
    ids_sem,
    acc_sem,
):
    bit = lax.axis_index("half").astype(jnp.int32)
    place = lax.rem(lax.axis_index("grp").astype(jnp.int32), BLOCK // slots)
    half_rows = own_ref.shape[1]
    width = own_ref.shape[2]
    senders = rows_ref.shape[0] // (slots + 1)
    stride = slots + 1
    per_half = half_rows // CHUNK
    blocks = CHUNK // BLOCK

    def fetch(src, chunk):
        return pltpu.make_async_copy(
            src.at[bit, pl.ds((chunk % per_half) * CHUNK, CHUNK), :],
            table.at[pl.ds(chunk * CHUNK, CHUNK), :],
            in_sem.at[chunk],
        )

    group = BLOCK // slots
    sector = lax.broadcasted_iota(jnp.int32, (senders // group, width), 1) // slots
    found = jnp.zeros((senders // group, width), jnp.float32)
    for part in range(group):
        ids = rows_ref[pl.ds(slots + part * stride, senders // group, stride=group * stride), :]
        ids = pltpu.roll(ids, lax.rem(part + group - place, group) * slots, 1)
        found = jnp.where(sector == part, ids, found)
    ids_v[...] = found.astype(jnp.int32)
    to_scalar = pltpu.make_async_copy(ids_v, ids_s, ids_sem)
    to_scalar.start()
    for top in range(2):
        for chunk in range(top * per_half, (top + 1) * per_half):

            @pl.when(bit == top)
            def _():
                fetch(own_ref, chunk).start()

            @pl.when(bit != top)
            def _():
                fetch(got_ref, chunk).start()

    zero = jnp.zeros((256, width), jnp.float32)

    def clear(step, carry):
        bank[pl.ds(pl.multiple_of(step * 256, 256), 256), :] = zero
        return carry

    lax.fori_loop(0, 2 * half_rows // 256, clear, 0)
    part = lax.broadcasted_iota(jnp.int32, spread_ref.shape, 0)
    column = lax.broadcasted_iota(jnp.int32, spread_ref.shape, 1)
    chosen = (part < 3 * blocks) & (part % blocks == column // BLOCK)
    spread_ref[...] = jnp.where(chosen, 1.0, 0.0).astype(jnp.bfloat16)
    to_scalar.wait()

    def gather(step, carry):
        for part in range(group):
            base = (step * group + part) * stride
            targets = [ids_s[step, part * slots + slot] for slot in range(slots)]
            held = [bank[pl.ds(target, 1), :] for target in targets]
            held = [old + rows_ref[pl.ds(base + slot, 1), :] for slot, old in enumerate(held)]
            for target, new in zip(targets, held):
                bank[pl.ds(target, 1), :] = new
        return carry

    for step in range(senders // group):
        gather(step, 0)

    lane = lax.broadcasted_iota(jnp.int32, (BLOCK, BLOCK), 1)
    def flush(chunk):
        return pltpu.make_async_copy(
            table.at[pl.ds(chunk * CHUNK, CHUNK), :],
            out_ref.at[pl.ds(chunk * CHUNK, CHUNK), :],
            out_sem.at[chunk],
        )

    def at(chunk, block):
        return pl.ds(pl.multiple_of(chunk * CHUNK + block * BLOCK, BLOCK), BLOCK)

    def measure(chunk):
        top = chunk // per_half
        step = chunk % per_half
        sums = jnp.zeros((BLOCK, BLOCK), jnp.float32)
        for block in range(blocks):
            value = bank[at(chunk, block), :]
            summed = jnp.sum(value * value, axis=1, keepdims=True)
            sums = jnp.where(lane == block, summed, sums)
        picked = pl.ds(2 * blocks * step + top, blocks, stride=2)
        state = acc_ref[picked, :]
        state = state + sums.T[:blocks, :] * (1.0 / width)
        states[picked, :] = state
        return LEARN_RATE / (jnp.sqrt(state) + EPSILON)

    def apply(chunk, scale):
        filler = jnp.zeros((BLOCK - 3 * blocks, BLOCK), jnp.float32)
        parts = [part.astype(jnp.float32) for part in split(scale)]
        parts = jnp.concatenate([*parts, filler], 0).T
        wide = jnp.dot(
            parts.astype(jnp.bfloat16), spread_ref[...], preferred_element_type=jnp.float32
        )
        for block in range(blocks):
            where = at(chunk, block)
            factor = wide[:, block * BLOCK : (block + 1) * BLOCK]
            table[where, :] = table[where, :] - bank[where, :] * factor

    def finish(chunk, scale):
        fetch(own_ref, chunk).wait()
        following = measure(chunk + 1)
        apply(chunk, scale)
        flush(chunk).start()
        return following

    last = 2 * per_half - 1
    scale = lax.fori_loop(0, last, finish, measure(0))
    states_out = pltpu.make_async_copy(states, out_acc_ref, acc_sem)
    states_out.start()
    fetch(own_ref, last).wait()
    apply(last, scale)
    flush(last).start()
    for chunk in range(2 * per_half):
        flush(chunk).wait()
    states_out.wait()


def update(own, got, acc, rows, slots):
    halves, half_rows, width = own.shape
    senders = rows.shape[0] // (slots + 1)
    chunks = halves * half_rows // CHUNK
    vmem = pl.BlockSpec(memory_space=pltpu.VMEM)
    hbm = pl.BlockSpec(memory_space=pltpu.HBM)
    return pl.pallas_call(
        functools.partial(update_kernel, slots),
        out_shape=(
            jax.ShapeDtypeStruct((halves * half_rows, width), jnp.float32),
            jax.ShapeDtypeStruct(acc.shape, jnp.float32),
        ),
        in_specs=[hbm, hbm, vmem, vmem],
        out_specs=(hbm, hbm),
        scratch_shapes=[
            pltpu.VMEM((halves * half_rows, width), jnp.float32),
            pltpu.VMEM((halves * half_rows + 8, width), jnp.float32),
            pltpu.VMEM(acc.shape, jnp.float32),
            pltpu.VMEM((senders * slots // width, width), jnp.int32),
            pltpu.SMEM((senders * slots // width, width), jnp.int32),
            pltpu.VMEM((BLOCK, CHUNK), jnp.bfloat16),
            pltpu.SemaphoreType.DMA((chunks,)),
            pltpu.SemaphoreType.DMA((chunks,)),
            pltpu.SemaphoreType.DMA,
            pltpu.SemaphoreType.DMA,
        ],
        compiler_params=pltpu.CompilerParams(vmem_limit_bytes=48 * 1024 * 1024),
        name="update",
    )(own, got, acc, rows)


def per_device(weights, accum, grads, row_ids, counts):
    owners, slots, width = grads.shape[1:]
    halves, half_rows = weights.shape[2:4]
    swap = [(0, 1), (1, 0)]
    table = weights[0, 0]
    bit = lax.axis_index("half").astype(jnp.int32)
    state = accum[0, 0].reshape(halves, half_rows // BLOCK, BLOCK).transpose(1, 0, 2)
    got = lax.ppermute(table, "half", swap)
    got_acc = lax.ppermute(state, "half", swap)
    packed = pack(grads[0], row_ids[0], counts, halves * half_rows)
    rows = lax.all_to_all(
        packed.reshape(owners, 1, (slots + 1) * width),
        ("half", "grp"),
        split_axis=0,
        concat_axis=0,
        tiled=True,
    ).reshape(owners * (slots + 1), width)
    mine = jnp.where(bit == 0, state[:, 0], state[:, 1])
    theirs = jnp.where(bit == 0, got_acc[:, 0], got_acc[:, 1])
    acc = jnp.stack([jnp.where(bit == 0, mine, theirs), jnp.where(bit == 0, theirs, mine)], 1)
    new_weights, new_accum = update(table, got, acc.reshape(-1, BLOCK), rows, slots)
    new_accum = new_accum.reshape(half_rows // BLOCK, halves, BLOCK).transpose(1, 0, 2)
    return (
        new_weights.reshape(1, 1, halves, half_rows, width),
        new_accum.reshape(1, 1, halves, half_rows),
    )


def solution(mesh):
    placed = (
        P("half", "grp", None, None, None),
        P("half", "grp", None, None),
        P(("half", "grp"), None, None, None),
        P(("half", "grp"), None, None),
        P(("half", "grp"), None),
    )
    return jax.shard_map(
        per_device,
        mesh=mesh,
        in_specs=placed,
        out_specs=(P("half", "grp", None, None, None), P("half", "grp", None, None)),
        check_vma=False,
    )
```

```python
import functools

import jax
import jax.numpy as jnp
from jax import lax
from jax.experimental import pallas as pl
from jax.experimental.pallas import tpu as pltpu
from jax.sharding import PartitionSpec as P

LEARN_RATE = 0.5
EPSILON = 1e-06
BLOCK = 128
CHUNK = 1024
PACK_STEPS = 4


def split(value):
    high = value.astype(jnp.bfloat16)
    rest = value - high.astype(jnp.float32)
    middle = rest.astype(jnp.bfloat16)
    low = (rest - middle.astype(jnp.float32)).astype(jnp.bfloat16)
    return high, middle, low


def pack_kernel(
    slots, dead, grads_ref, ids_hbm, counts_hbm, out_ref, grads, packed, turned, flat, merges, kepts,
    ids_ref, counts_ref, in_sem, out_sem, ids_sem
):
    owners = ids_ref.shape[1]
    stride = slots + 1
    group = BLOCK // slots
    batches = grads.shape[0] // BLOCK // PACK_STEPS
    made = batches * group * stride

    def fetch():
        return pltpu.make_async_copy(grads_ref, grads, in_sem)

    def flush(step):
        where = pl.ds(step * made, made)
        return pltpu.make_async_copy(packed.at[where, :], out_ref.at[where, :], out_sem.at[step])

    small = [
        pltpu.make_async_copy(ids_hbm, ids_ref, ids_sem.at[0]),
        pltpu.make_async_copy(counts_hbm, counts_ref, ids_sem.at[1]),
    ]
    for copy in small:
        copy.start()
    fetch().start()
    for copy in small:
        copy.wait()
    slot = lax.broadcasted_iota(jnp.int32, ids_ref.shape, 0)
    marked = jnp.where(slot < counts_ref[...], ids_ref[...], dead).astype(jnp.float32)
    filler = jnp.zeros((BLOCK - slots, owners), jnp.float32)
    turned[...] = jnp.concatenate([marked, filler], 0).T
    rows = turned[pl.ds(0, owners // group, stride=group), :]
    for part in range(1, group):
        piece = turned[pl.ds(part, owners // group, stride=group), :]
        rows = rows + pltpu.roll(piece, part * slots, 1)
    flat[...] = rows

    below = lax.broadcasted_iota(jnp.int32, (BLOCK, BLOCK), 0)
    across = lax.broadcasted_iota(jnp.int32, (BLOCK, BLOCK), 1)
    together = below // slots == across // slots
    earlier = together & (below < across)
    for batch in range(batches * PACK_STEPS):
        row = flat[batch : batch + 1, :]
        wide = jnp.broadcast_to(row, (BLOCK, BLOCK))
        same = wide == wide.T
        merges[batch * BLOCK : (batch + 1) * BLOCK, :] = jnp.where(
            same & together, 1.0, 0.0
        ).astype(jnp.bfloat16)
        seen = jnp.max(jnp.where(same & earlier, 1.0, 0.0), axis=0, keepdims=True)
        kepts[batch : batch + 1, :] = jnp.where(seen > 0, float(dead), row)
    fetch().wait()
    for batch in range(batches * PACK_STEPS):
        merge = merges[batch * BLOCK : (batch + 1) * BLOCK, :]
        kept = kepts[batch : batch + 1, :]
        merged = jnp.zeros((BLOCK, BLOCK), jnp.float32)
        for part in split(grads[batch * BLOCK : (batch + 1) * BLOCK, :]):
            merged = merged + jnp.dot(merge, part, preferred_element_type=jnp.float32)
        for owner in range(group):
            base = stride * (batch * group + owner)
            packed[base : base + slots, :] = merged[owner * slots : (owner + 1) * slots, :]
            packed[base + slots : base + stride, :] = kept
        if batch % batches == batches - 1:
            flush(batch // batches).start()
    for step in range(PACK_STEPS):
        flush(step).wait()


def pack(grads, ids, counts, dead):
    owners, slots, width = grads.shape
    made = owners * (slots + 1)
    hbm = pl.BlockSpec(memory_space=pltpu.HBM)
    return pl.pallas_call(
        functools.partial(pack_kernel, slots, dead),
        out_shape=jax.ShapeDtypeStruct((made, width), jnp.float32),
        in_specs=[hbm, hbm, hbm],
        out_specs=hbm,
        scratch_shapes=[
            pltpu.VMEM((owners * slots, width), jnp.float32),
            pltpu.VMEM((made, width), jnp.float32),
            pltpu.VMEM((owners, BLOCK), jnp.float32),
            pltpu.VMEM((owners * slots // BLOCK, BLOCK), jnp.float32),
            pltpu.VMEM((owners * slots, BLOCK), jnp.bfloat16),
            pltpu.VMEM((owners * slots // BLOCK, BLOCK), jnp.float32),
            pltpu.VMEM((slots, owners), jnp.int32),
            pltpu.VMEM((1, owners), jnp.int32),
            pltpu.SemaphoreType.DMA,
            pltpu.SemaphoreType.DMA((PACK_STEPS,)),
            pltpu.SemaphoreType.DMA((2,)),
        ],
        name="pack",
    )(grads.reshape(owners * slots, width), ids.T, counts)


def update_kernel(
    slots,
    own_ref,
    got_ref,
    acc_ref,
    rows_ref,
    out_ref,
    out_acc_ref,
    table,
    bank,
    states,
    ids_v,
    ids_s,
    spread_ref,
    in_sem,
    out_sem,
    ids_sem,
    acc_sem,
):
    bit = lax.axis_index("half").astype(jnp.int32)
    place = lax.rem(lax.axis_index("grp").astype(jnp.int32), BLOCK // slots)
    half_rows = own_ref.shape[1]
    width = own_ref.shape[2]
    senders = rows_ref.shape[0] // (slots + 1)
    stride = slots + 1
    per_half = half_rows // CHUNK
    blocks = CHUNK // BLOCK

    def fetch(src, chunk):
        return pltpu.make_async_copy(
            src.at[bit, pl.ds((chunk % per_half) * CHUNK, CHUNK), :],
            table.at[pl.ds(chunk * CHUNK, CHUNK), :],
            in_sem.at[chunk],
        )

    group = BLOCK // slots
    sector = lax.broadcasted_iota(jnp.int32, (senders // group, width), 1) // slots
    found = jnp.zeros((senders // group, width), jnp.float32)
    for part in range(group):
        ids = rows_ref[pl.ds(slots + part * stride, senders // group, stride=group * stride), :]
        ids = pltpu.roll(ids, lax.rem(part + group - place, group) * slots, 1)
        found = jnp.where(sector == part, ids, found)
    ids_v[...] = found.astype(jnp.int32)
    to_scalar = pltpu.make_async_copy(ids_v, ids_s, ids_sem)
    to_scalar.start()
    for top in range(2):
        for chunk in range(top * per_half, (top + 1) * per_half):

            @pl.when(bit == top)
            def _():
                fetch(own_ref, chunk).start()

            @pl.when(bit != top)
            def _():
                fetch(got_ref, chunk).start()

    zero = jnp.zeros((256, width), jnp.float32)

    def clear(step, carry):
        bank[pl.ds(pl.multiple_of(step * 256, 256), 256), :] = zero
        return carry

    lax.fori_loop(0, 2 * half_rows // 256, clear, 0)
    part = lax.broadcasted_iota(jnp.int32, spread_ref.shape, 0)
    column = lax.broadcasted_iota(jnp.int32, spread_ref.shape, 1)
    chosen = (part < 3 * blocks) & (part % blocks == column // BLOCK)
    spread_ref[...] = jnp.where(chosen, 1.0, 0.0).astype(jnp.bfloat16)
    to_scalar.wait()

    def gather(step, carry):
        for part in range(group):
            base = (step * group + part) * stride
            targets = [ids_s[step, part * slots + slot] for slot in range(slots)]
            held = [bank[pl.ds(target, 1), :] for target in targets]
            held = [old + rows_ref[pl.ds(base + slot, 1), :] for slot, old in enumerate(held)]
            for target, new in zip(targets, held):
                bank[pl.ds(target, 1), :] = new
        return carry

    for step in range(senders // group):
        gather(step, 0)

    lane = lax.broadcasted_iota(jnp.int32, (BLOCK, BLOCK), 1)
    def flush(chunk):
        return pltpu.make_async_copy(
            table.at[pl.ds(chunk * CHUNK, CHUNK), :],
            out_ref.at[pl.ds(chunk * CHUNK, CHUNK), :],
            out_sem.at[chunk],
        )

    def at(chunk, block):
        return pl.ds(pl.multiple_of(chunk * CHUNK + block * BLOCK, BLOCK), BLOCK)

    def measure(chunk):
        top = chunk // per_half
        step = chunk % per_half
        sums = jnp.zeros((BLOCK, BLOCK), jnp.float32)
        for block in range(blocks):
            value = bank[at(chunk, block), :]
            summed = jnp.sum(value * value, axis=1, keepdims=True)
            sums = jnp.where(lane == block, summed, sums)
        picked = pl.ds(2 * blocks * step + top, blocks, stride=2)
        state = acc_ref[picked, :]
        state = state + sums.T[:blocks, :] * (1.0 / width)
        states[picked, :] = state
        return LEARN_RATE / (jnp.sqrt(state) + EPSILON)

    def apply(chunk, scale):
        filler = jnp.zeros((BLOCK - 3 * blocks, BLOCK), jnp.float32)
        parts = [part.astype(jnp.float32) for part in split(scale)]
        parts = jnp.concatenate([*parts, filler], 0).T
        wide = jnp.dot(
            parts.astype(jnp.bfloat16), spread_ref[...], preferred_element_type=jnp.float32
        )
        for block in range(blocks):
            where = at(chunk, block)
            factor = wide[:, block * BLOCK : (block + 1) * BLOCK]
            table[where, :] = table[where, :] - bank[where, :] * factor

    def finish(chunk, scale):
        fetch(own_ref, chunk).wait()
        following = measure(chunk + 1)
        apply(chunk, scale)
        flush(chunk).start()
        return following

    last = 2 * per_half - 1
    scale = lax.fori_loop(0, last, finish, measure(0))
    states_out = pltpu.make_async_copy(states, out_acc_ref, acc_sem)
    states_out.start()
    fetch(own_ref, last).wait()
    apply(last, scale)
    flush(last).start()
    for chunk in range(2 * per_half):
        flush(chunk).wait()
    states_out.wait()


def update(own, got, acc, rows, slots):
    halves, half_rows, width = own.shape
    senders = rows.shape[0] // (slots + 1)
    chunks = halves * half_rows // CHUNK
    vmem = pl.BlockSpec(memory_space=pltpu.VMEM)
    hbm = pl.BlockSpec(memory_space=pltpu.HBM)
    return pl.pallas_call(
        functools.partial(update_kernel, slots),
        out_shape=(
            jax.ShapeDtypeStruct((halves * half_rows, width), jnp.float32),
            jax.ShapeDtypeStruct(acc.shape, jnp.float32),
        ),
        in_specs=[hbm, hbm, vmem, vmem],
        out_specs=(hbm, hbm),
        scratch_shapes=[
            pltpu.VMEM((halves * half_rows, width), jnp.float32),
            pltpu.VMEM((halves * half_rows + 8, width), jnp.float32),
            pltpu.VMEM(acc.shape, jnp.float32),
            pltpu.VMEM((senders * slots // width, width), jnp.int32),
            pltpu.SMEM((senders * slots // width, width), jnp.int32),
            pltpu.VMEM((BLOCK, CHUNK), jnp.bfloat16),
            pltpu.SemaphoreType.DMA((chunks,)),
            pltpu.SemaphoreType.DMA((chunks,)),
            pltpu.SemaphoreType.DMA,
            pltpu.SemaphoreType.DMA,
        ],
        compiler_params=pltpu.CompilerParams(vmem_limit_bytes=48 * 1024 * 1024),
        name="update",
    )(own, got, acc, rows)


def per_device(weights, accum, grads, row_ids, counts):
    owners, slots, width = grads.shape[1:]
    halves, half_rows = weights.shape[2:4]
    swap = [(0, 1), (1, 0)]
    table = weights[0, 0]
    bit = lax.axis_index("half").astype(jnp.int32)
    state = accum[0, 0].reshape(halves, half_rows // BLOCK, BLOCK).transpose(1, 0, 2)
    got = lax.ppermute(table, "half", swap)
    got_acc = lax.ppermute(state, "half", swap)
    packed = pack(grads[0], row_ids[0], counts, halves * half_rows)
    rows = lax.all_to_all(
        packed.reshape(owners, 1, (slots + 1) * width),
        ("half", "grp"),
        split_axis=0,
        concat_axis=0,
        tiled=True,
    ).reshape(owners * (slots + 1), width)
    mine = jnp.where(bit == 0, state[:, 0], state[:, 1])
    theirs = jnp.where(bit == 0, got_acc[:, 0], got_acc[:, 1])
    acc = jnp.stack([jnp.where(bit == 0, mine, theirs), jnp.where(bit == 0, theirs, mine)], 1)
    new_weights, new_accum = update(table, got, acc.reshape(-1, BLOCK), rows, slots)
    new_accum = new_accum.reshape(half_rows // BLOCK, halves, BLOCK).transpose(1, 0, 2)
    return (
        new_weights.reshape(1, 1, halves, half_rows, width),
        new_accum.reshape(1, 1, halves, half_rows),
    )


def solution(mesh):
    placed = (
        P("half", "grp", None, None, None),
        P("half", "grp", None, None),
        P(("half", "grp"), None, None, None),
        P(("half", "grp"), None, None),
        P(("half", "grp"), None),
    )
    return jax.shard_map(
        per_device,
        mesh=mesh,
        in_specs=placed,
        out_specs=(P("half", "grp", None, None, None), P("half", "grp", None, None)),
        check_vma=False,
    )
```
